32 devices in a mesh: fsdp: 8 (over z, y), ctx: 2 (over x), tp: 2 (over core).
Axes of the slice: x: 2, y: 2, z: 4, core: 2. Of those that a mesh axis runs over, the one named last changes fastest.
Arguments:
- inputs: bfloat16 [8, 1408, 1024], P('fsdp', 'ctx', 'tp'), may hold values from -6 to 6
- w_qkv: bfloat16 [3, 1024, 1024], P(None, 'fsdp', 'tp'), may hold values from -3.28125 to 3.28125
- b_qv: bfloat16 [2, 1024], P(None, 'tp'), may hold values from -3 to 3
- w_out: bfloat16 [1024, 1024], P('fsdp', 'tp'), may hold values from -0.375 to 0.375
- b_out: bfloat16 [1024], P('tp'), may hold values from -3 to 3
- ln1_gain: bfloat16 [1024], replicated, may hold values from 0.25 to 1.75
- ln1_bias: bfloat16 [1024], replicated, may hold values from -2 to 2
- ln2_gain: bfloat16 [1024], replicated, may hold values from 0.25 to 1.75
- ln2_bias: bfloat16 [1024], replicated, may hold values from -2 to 2
- w_fc1: bfloat16 [1024, 4096], P('fsdp', 'tp'), may hold values from -0.1875 to 0.1875
- b_fc1: bfloat16 [4096], P('tp'), may hold values from -3 to 3
- w_fc2: bfloat16 [1024, 4096], P('fsdp', 'tp'), may hold values from -0.09375 to 0.09375
- b_fc2: bfloat16 [1024], P('tp'), may hold values from -3 to 3
- ls1: bfloat16 [1024], P('tp'), may hold values from 0.29882812 to 1.5
- ls2: bfloat16 [1024], P('tp'), may hold values from 0.29882812 to 1.5
- lengths: int32 [8], P('fsdp'), may hold values from 1232 to 1408
- out_grad: bfloat16 [8, 1408, 1024], P('fsdp', 'ctx', 'tp'), may hold values from -6 to 6
Outputs:
- result: bfloat16 [8, 1408, 1024], P('fsdp', 'ctx', 'tp')
- in_grad: bfloat16 [8, 1408, 1024], P('fsdp', 'ctx', 'tp')
- w_qkv_grad: float32 [3, 1024, 1024], P(None, 'fsdp', 'tp')
- b_qv_grad: float32 [2, 1024], P(None, 'tp')
- w_out_grad: float32 [1024, 1024], P('fsdp', 'tp')
- b_out_grad: float32 [1024], P('tp')
- ln1_gain_grad: float32 [1024], replicated
- ln1_bias_grad: float32 [1024], replicated
- ln2_gain_grad: float32 [1024], replicated
- ln2_bias_grad: float32 [1024], replicated
- w_fc1_grad: float32 [1024, 4096], P('fsdp', 'tp')
- b_fc1_grad: float32 [4096], P('tp')
- w_fc2_grad: float32 [1024, 4096], P('fsdp', 'tp')
- b_fc2_grad: float32 [1024], P('tp')
- ls1_grad: float32 [1024], P('tp')
- ls2_grad: float32 [1024], P('tp')
The draws below stay inside these ranges and needn't reach their ends.
Inputs may be any that keep to these rules, and one draw needn't show every extreme that they name: Token slots from lengths[image] on are padding; keys there are masked.
All inputs are finite; a program needn't handle non-finite values.
Results may differ from the reference program's by a relative error of at most 0.028.
The reference program's roundings to bfloat16 on the way count: a program that leaves them out, or rounds other values in their place, can miss the bound.
Values may be sent and summed in bfloat16 or wider, within the bound.
No kernel may reach another device: no remote copies, remote signals or barrier semaphores. Data moves between devices by JAX's collectives and lax.ppermute only.
A program may use at most 192 MiB of HBM per device.

```python
import math
import jax
import jax.numpy as jnp
from jax import lax

D = 1024
HEADS = 16
HD = 64
FF = 4096
SEQ = 1408
IMAGES = 8


def draw_w_qkv(key, part):
    first = jax.random.fold_in(jax.random.fold_in(key, 7301), 0)
    base = jnp.clip(jax.random.normal(first, (3, D, D), jnp.float32), -5.0, 5.0) * D ** (-0.5)
    return base.astype(jnp.bfloat16)


def with_ends(values, stream_key, low, high):
    longest = values.shape.index(max(values.shape))
    spots = []
    for shift in (0, 1):
        where = [jax.random.randint(jax.random.fold_in(stream_key, axis), (), 0, length) for axis, length in enumerate(values.shape)]
        where[longest] = (where[longest] + shift) % values.shape[longest]
        spots.append(tuple(where))
    return values.at[spots[0]].set(low).at[spots[1]].set(high)


def raised(entries, stream_key, source, target, parts, factor):
    def block_of(position):
        return (jnp.arange(entries.shape[position]) // (entries.shape[position] // parts)).reshape((-1,) + (1,) * (entries.ndim - 1 - position))

    first = jax.random.permutation(stream_key, parts)[block_of(target)]
    far = (block_of(target) + parts // 2) % parts
    return jnp.where((block_of(source) == first) | (block_of(source) == far), factor * entries, entries)


def block_levels(key, dims, shards, smallest, top_value):
    def one(position, shards_of):
        draws = jax.random.uniform(jax.random.fold_in(jax.random.fold_in(key, 6), position), (shards_of,), jnp.float32, smallest / len(shards), top_value / len(shards))
        return jnp.repeat(jnp.exp(draws), dims[position] // shards_of).reshape((-1,) + (1,) * (len(dims) - position - 1))

    level = one(*shards[0])
    for cut in shards[1:]:
        level = level * one(*cut)
    return level


def normal_values(key, shape, width, limit, cuts=(), kind=jnp.bfloat16):
    drawn = width * jax.random.normal(key, shape, jnp.float32)
    if cuts:
        drawn = drawn * block_levels(key, shape, cuts, -0.22, 0.18)
    return jnp.clip(drawn, -limit, limit).astype(kind)


def heavy_noise(stream_key, dims, width, reach, pieces, heavy, held_as=jnp.bfloat16):
    drawn = width * jax.random.normal(stream_key, dims, jnp.float32)
    if pieces:
        drawn = drawn * block_levels(stream_key, dims, pieces, -0.22, 0.18)
    return jnp.clip(raised(drawn, jax.random.fold_in(stream_key, 3), *heavy), -reach, reach).astype(held_as)


def setup_inputs(seed: int = 0) -> dict:
    keys = jax.random.split(jax.random.key(seed), 18)
    return {
        "inputs": normal_values(keys[0], (IMAGES, SEQ, D), 1.0, 6.0, ((0, 8), (1, 2), (2, 2))),
        "w_qkv": draw_w_qkv(jax.random.fold_in(keys[17], 71), 0),
        "b_qv": normal_values(keys[2], (2, D), 0.5, 3.0, ((1, 2),)),
        "w_out": normal_values(keys[3], (D, D), (D // 4) ** -0.5, 0.375, ((0, 8), (1, 2))),
        "b_out": normal_values(keys[4], (D,), 0.5, 3.0, ((0, 2),)),
        "ln1_gain": jnp.clip(1.0 + 0.15 * jax.random.normal(keys[5], (D,), jnp.float32), 0.25, 1.75).astype(jnp.bfloat16),
        "ln1_bias": normal_values(keys[6], (D,), 0.3, 2.0),
        "ln2_gain": jnp.clip(1.0 + 0.15 * jax.random.normal(keys[7], (D,), jnp.float32), 0.25, 1.75).astype(jnp.bfloat16),
        "ln2_bias": normal_values(keys[8], (D,), 0.3, 2.0),
        "w_fc1": normal_values(keys[9], (D, FF), D ** -0.5, 0.1875, ((0, 8), (1, 2))),
        "b_fc1": normal_values(keys[10], (FF,), 0.5, 3.0, ((0, 2),)),
        "w_fc2": normal_values(keys[11], (D, FF), FF ** -0.5, 0.09375, ((0, 8), (1, 2))),
        "b_fc2": normal_values(keys[12], (D,), 0.5, 3.0, ((0, 2),)),
        "ls1": jnp.clip(jnp.exp(math.log(1.5) - 1.6133518 * jax.random.uniform(keys[13], (D,), jnp.float32) ** block_levels(keys[13], (D,), ((0, 2),), -0.2, 0.2)), 0.29882812, 1.5).astype(jnp.bfloat16),
        "ls2": jnp.clip(jnp.exp(math.log(1.5) - 1.6133518 * jax.random.uniform(keys[14], (D,), jnp.float32) ** block_levels(keys[14], (D,), ((0, 2),), -0.2, 0.2)), 0.29882812, 1.5).astype(jnp.bfloat16),
        "lengths": with_ends(jax.random.randint(keys[15], (IMAGES,), SEQ - SEQ // 8, SEQ + 1), jax.random.fold_in(keys[15], 1), SEQ - SEQ // 8, SEQ).astype(jnp.int32),
        "out_grad": heavy_noise(keys[16], (IMAGES, SEQ, D), 1.0, 6.0, ((0, 8), (1, 2), (2, 2)), (0, 2, 8, 2.0)),
    }


norm_eps = 1e-06
root_half = 0.7071067811865476
inv_root_two_pi = 0.3989422804014327

def normalize(values):
    average = lax.optimization_barrier(jnp.mean(values, axis=-1, keepdims=True))
    centred = values - average
    inv_std = lax.rsqrt(lax.optimization_barrier(jnp.mean(centred * centred, axis=-1, keepdims=True)) + norm_eps)
    return (centred * inv_std, inv_std)

def normalize_back(grad_normed, normed, inv_std):
    first = lax.optimization_barrier(jnp.mean(grad_normed, axis=-1, keepdims=True))
    second = lax.optimization_barrier(jnp.mean(grad_normed * normed, axis=-1, keepdims=True))
    return inv_std * (grad_normed - first - normed * second)

def gelu_slope(pre):
    return 0.5 * (1.0 + jax.scipy.special.erf(pre * root_half)) + pre * inv_root_two_pi * jnp.exp(-0.5 * pre * pre)

def reference(inputs, w_qkv, b_qv, w_out, b_out, ln1_gain, ln1_bias, ln2_gain, ln2_bias, w_fc1, b_fc1, w_fc2, b_fc2, ls1, ls2, lengths, out_grad):
    single = jnp.float32
    half = jnp.bfloat16
    softmax_scale = HD ** (-0.5)
    qkv_wide = w_qkv.astype(single)
    gain1 = ln1_gain.astype(single)
    gain2 = ln2_gain.astype(single)
    scale1 = ls1.astype(single)
    scale2 = ls2.astype(single)

    def one_image(totals, slices):
        image, grad_out, length = slices
        xin = image.astype(single)
        normed1, inv1 = normalize(xin)
        act1 = (normed1 * gain1 + ln1_bias.astype(single)).astype(half)
        query_rows = ((jnp.dot(act1, w_qkv[0], preferred_element_type=single) + b_qv[0].astype(single)) * softmax_scale).astype(half)
        key_rows = jnp.dot(act1, w_qkv[1], preferred_element_type=single).astype(half)
        value_rows = (jnp.dot(act1, w_qkv[2], preferred_element_type=single) + b_qv[1].astype(single)).astype(half)
        query_heads = query_rows.astype(single).reshape(SEQ, HEADS, HD)
        key_heads = key_rows.astype(single).reshape(SEQ, HEADS, HD)
        value_heads = value_rows.astype(single).reshape(SEQ, HEADS, HD)
        scores = jnp.einsum('shd,phd->hsp', query_heads, key_heads)
        live_keys = (jnp.arange(SEQ, dtype=jnp.int32) < length)[None, None, :]
        scores = jnp.where(live_keys, scores, -1e+30)
        top = lax.optimization_barrier(jnp.max(scores, axis=-1, keepdims=True))
        total = lax.optimization_barrier(jnp.sum(jnp.where(live_keys, jnp.exp(scores - top), 0.0), axis=-1, keepdims=True))
        log_total = top + jnp.log(total)
        probs = jnp.where(live_keys, jnp.exp(scores - log_total), 0.0)
        probs_half = lax.optimization_barrier(probs.astype(half)).astype(single)
        attn = jnp.einsum('hsp,phd->shd', probs, value_heads).reshape(SEQ, D).astype(half)
        attn_proj = jnp.dot(attn, w_out.T, preferred_element_type=single) + b_out.astype(single)
        hidden1 = (xin + scale1 * attn_proj).astype(half)
        hidden_wide = hidden1.astype(single)
        normed2, inv2 = normalize(hidden_wide)
        act2 = (normed2 * gain2 + ln2_bias.astype(single)).astype(half)
        pre = jnp.dot(act2, w_fc1, preferred_element_type=single) + b_fc1.astype(single)
        inner = jax.nn.gelu(pre, approximate=False).astype(half)
        mlp = jnp.dot(inner, w_fc2.T, preferred_element_type=single) + b_fc2.astype(single)
        result = (hidden_wide + scale2 * mlp).astype(half)
        grad_y = grad_out.astype(single)
        g_ls2 = lax.optimization_barrier(jnp.sum(grad_y * mlp, axis=0))
        g_bfc2 = lax.optimization_barrier(jnp.sum(grad_y * scale2, axis=0))
        grad_mlp = (grad_y * scale2).astype(half)
        grad_inner = jnp.dot(grad_mlp, w_fc2, preferred_element_type=single)
        g_wfc2 = jnp.dot(grad_mlp.T, inner, preferred_element_type=single)
        grad_pre = grad_inner * gelu_slope(pre)
        g_bfc1 = lax.optimization_barrier(jnp.sum(grad_pre, axis=0))
        grad_pre_half = grad_pre.astype(half)
        g_wfc1 = jnp.dot(act2.T, grad_pre_half, preferred_element_type=single)
        grad_act2 = jnp.dot(grad_pre_half, w_fc1.T, preferred_element_type=single)
        g_ln2g = lax.optimization_barrier(jnp.sum(grad_act2 * normed2, axis=0))
        g_ln2b = lax.optimization_barrier(jnp.sum(grad_act2, axis=0))
        grad_h1 = grad_y + normalize_back(grad_act2 * gain2, normed2, inv2)
        g_ls1 = lax.optimization_barrier(jnp.sum(grad_h1 * attn_proj, axis=0))
        g_bout = lax.optimization_barrier(jnp.sum(grad_h1 * scale1, axis=0))
        grad_proj = (grad_h1 * scale1).astype(half)
        g_wout = jnp.dot(grad_proj.T, attn, preferred_element_type=single)
        grad_attn = jnp.dot(grad_proj, w_out, preferred_element_type=single).astype(half)
        grad_heads = grad_attn.astype(single).reshape(SEQ, HEADS, HD)
        attn_heads = attn.astype(single).reshape(SEQ, HEADS, HD)
        row_dots = jnp.einsum('shd,shd->hs', grad_heads, attn_heads)
        grad_value_heads = jnp.einsum('hsp,shd->phd', probs_half, grad_heads)
        grad_probs = jnp.einsum('shd,phd->hsp', grad_heads, value_heads)
        grad_scores = lax.optimization_barrier((probs * (grad_probs - row_dots[:, :, None])).astype(half)).astype(single)
        grad_query = jnp.einsum('hsp,phd->shd', grad_scores, key_heads).reshape(SEQ, D) * softmax_scale
        grad_key = jnp.einsum('hsp,shd->phd', grad_scores, query_heads).reshape(SEQ, D)
        grad_value = grad_value_heads.reshape(SEQ, D)
        g_bqv = jnp.stack([lax.optimization_barrier(jnp.sum(grad_query, axis=0)), lax.optimization_barrier(jnp.sum(grad_value, axis=0))])
        grad_qkv = jnp.stack([grad_query, grad_key, grad_value]).astype(half).astype(single)
        g_wqkv = jnp.einsum('sd,cse->cde', act1.astype(single), grad_qkv)
        grad_act1 = jnp.einsum('cse,cde->sd', grad_qkv, qkv_wide)
        g_ln1g = lax.optimization_barrier(jnp.sum(grad_act1 * normed1, axis=0))
        g_ln1b = lax.optimization_barrier(jnp.sum(grad_act1, axis=0))
        in_grad = (grad_h1 + normalize_back(grad_act1 * gain1, normed1, inv1)).astype(half)
        terms = (g_wqkv, g_bqv, g_wout, g_bout, g_ln1g, g_ln1b, g_ln2g, g_ln2b, g_wfc1, g_bfc1, g_wfc2, g_bfc2, g_ls1, g_ls2)
        totals = tuple((left + right for left, right in zip(totals, terms)))
        return (totals, (result, in_grad))
    start_totals = (jnp.zeros((3, D, D), single), jnp.zeros((2, D), single), jnp.zeros((D, D), single), jnp.zeros((D,), single), jnp.zeros((D,), single), jnp.zeros((D,), single), jnp.zeros((D,), single), jnp.zeros((D,), single), jnp.zeros((D, FF), single), jnp.zeros((FF,), single), jnp.zeros((D, FF), single), jnp.zeros((D,), single), jnp.zeros((D,), single), jnp.zeros((D,), single))
    totals, outputs = lax.scan(one_image, start_totals, (inputs, out_grad, lengths.astype(jnp.int32)))
    g_wqkv, g_bqv, g_wout, g_bout, g_ln1g, g_ln1b, g_ln2g, g_ln2b, g_wfc1, g_bfc1, g_wfc2, g_bfc2, g_ls1, g_ls2 = totals
    return (outputs[0], outputs[1], g_wqkv, g_bqv, g_wout, g_bout, g_ln1g, g_ln1b, g_ln2g, g_ln2b, g_wfc1, g_bfc1, g_wfc2, g_bfc2, g_ls1, g_ls2)
```

```python
import jax
import jax.numpy as jnp
from jax import lax
from jax.sharding import PartitionSpec as P

HD = 64
norm_eps = 1e-06
root_half = 0.7071067811865476
inv_root_two_pi = 0.3989422804014327
single = jnp.float32
half = jnp.bfloat16


def normalize(values):
    average = jnp.mean(values, axis=-1, keepdims=True)
    centred = values - average
    inv_std = lax.rsqrt(jnp.mean(centred * centred, axis=-1, keepdims=True) + norm_eps)
    return (centred * inv_std, inv_std)


def normalize_back(grad_normed, normed, inv_std):
    first = jnp.mean(grad_normed, axis=-1, keepdims=True)
    second = jnp.mean(grad_normed * normed, axis=-1, keepdims=True)
    return inv_std * (grad_normed - first - normed * second)


def gelu_slope(pre):
    return 0.5 * (1.0 + jax.scipy.special.erf(pre * root_half)) + pre * inv_root_two_pi * jnp.exp(
        -0.5 * pre * pre
    )


def dot(left, right, dims):
    return lax.dot_general(left, right, (dims, ((), ())), preferred_element_type=single)


def make_body(n_fsdp, n_ctx):
    n_line = n_fsdp // 2

    def line_perm(step):
        return [
            (((line + step) % n_line) * 2 + pair, line * 2 + pair)
            for line in range(n_line)
            for pair in range(2)
        ]

    def pair_swap(values):
        return lax.ppermute(values, "fsdp", [(i, i ^ 1) for i in range(n_fsdp)])

    def from_line(values, step):
        return lax.ppermute(values, "fsdp", line_perm(step))

    def tp_swap(values):
        return lax.ppermute(values, "tp", [(0, 1), (1, 0)])

    def from_ctx(values, step):
        return lax.ppermute(values, "ctx", [((i + step) % n_ctx, i) for i in range(n_ctx)])

    def doubling(values, axis, count, link):
        step = 1
        while step < count:
            sent = values.astype(link)
            other = lax.ppermute(sent, axis, [(i, i ^ step) for i in range(count)])
            values = sent.astype(single) + other.astype(single)
            step *= 2
        return values

    def line_order():
        steps = list(range(1, n_line))
        return sorted(steps, key=lambda s: min(s, n_line - s))

    def gather_rows(shard, axis):
        blocks = {0: shard}
        swapped = {0: pair_swap(shard)}
        for step in line_order():
            blocks[step] = from_line(shard, step)
        for step in line_order():
            swapped[step] = pair_swap(blocks[step])
        return lax.concatenate(
            [blocks[s] for s in range(n_line)] + [swapped[s] for s in range(n_line)], axis
        )

    def scatter_rows(make_half, axis):
        sent = make_half(1).astype(half)
        came = pair_swap(sent).astype(single)
        kept = make_half(0)
        mixed = kept + came
        rows = mixed.shape[axis] // n_line
        own = lax.slice_in_dim(mixed, 0, rows, axis=axis)
        for step in line_order():
            part = lax.slice_in_dim(mixed, step * rows, (step + 1) * rows, axis=axis).astype(half)
            own = own + from_line(part, n_line - step).astype(single)
        return doubling(own, "ctx", n_ctx, half)

    def swap_sum(left, right, dims):
        rows = left.shape[0]
        cut = (rows // 2 + 15) // 16 * 16
        parts = [dot(left[:cut], right, dims), dot(left[cut:], right, dims)]
        others = [tp_swap(part) for part in parts]
        return jnp.concatenate([a + b for a, b in zip(parts, others)], axis=0)

    def body(
        inputs, w_qkv, b_qv, w_out, b_out, ln1_gain, ln1_bias, ln2_gain, ln2_bias,
        w_fc1, b_fc1, w_fc2, b_fc2, ls1, ls2, lengths, out_grad,
    ):
        seq_rows, width_part = inputs.shape[1], inputs.shape[2]
        width = 2 * width_part
        heads_part = width_part // HD
        softmax_scale = HD ** (-0.5)
        tp_index = lax.axis_index("tp")
        ctx_index = lax.axis_index("ctx")
        place = lax.axis_index("fsdp")
        line, pair = place // 2, place % 2

        full_qkv = gather_rows(w_qkv, 1)
        full_out = gather_rows(w_out, 0)
        full_fc1 = gather_rows(w_fc1, 0)
        full_fc2 = gather_rows(w_fc2, 0)

        slot = jnp.arange(width, dtype=jnp.int32)
        block_rows = width // n_fsdp
        block = slot // block_rows
        owner = ((line + block % n_line) % n_line) * 2 + (pair ^ (block // n_line))
        feature = owner * block_rows + slot % block_rows
        own_first = (slot + tp_index * width_part) % width
        select = (own_first[:, None] == feature[None, :]).astype(half)

        def to_device_order(own):
            both = jnp.concatenate([own, tp_swap(own)], axis=1)
            return dot(both, select, ((1,), (0,)))

        def own_features(values):
            return dot(values, select[:width_part], ((1,), (1,))).astype(half)

        x_full = to_device_order(inputs[0])
        grad_y = to_device_order(out_grad[0])
        small_own = to_device_order(jnp.stack([b_out, b_fc2, ls1, ls2]))
        bias_out, bias_fc2, scale1, scale2 = [small_own[i : i + 1] for i in range(4)]
        plain = (slot[:, None] == feature[None, :]).astype(half)
        small_all = dot(
            jnp.stack([ln1_gain, ln1_bias, ln2_gain, ln2_bias]), plain, ((1,), (0,))
        )
        gain1, shift1, gain2, shift2 = [small_all[i : i + 1] for i in range(4)]

        normed1, inv1 = normalize(x_full)
        act1 = (normed1 * gain1 + shift1).astype(half)
        query_rows = (
            (dot(act1, full_qkv[0], ((1,), (0,))) + b_qv[0].astype(single)) * softmax_scale
        ).astype(half)
        key_rows = dot(act1, full_qkv[1], ((1,), (0,))).astype(half)
        value_rows = (dot(act1, full_qkv[2], ((1,), (0,))) + b_qv[1].astype(single)).astype(half)
        query_heads = query_rows.reshape(seq_rows, heads_part, HD)

        own_kv = jnp.stack([key_rows, value_rows])
        kv = jnp.concatenate(
            [own_kv] + [from_ctx(own_kv, step) for step in range(1, n_ctx)], axis=1
        )
        count = n_ctx * seq_rows
        key_heads = kv[0].reshape(count, heads_part, HD)
        value_heads = kv[1].reshape(count, heads_part, HD)
        at = jnp.arange(count, dtype=jnp.int32)
        positions = ((ctx_index + at // seq_rows) % n_ctx) * seq_rows + at % seq_rows
        live_keys = (positions < lengths[0])[None, None, :]

        def all_scores(queries, keys):
            scores = jnp.einsum("shd,phd->hsp", queries, keys, preferred_element_type=single)
            return jnp.where(live_keys, scores, -1e30)

        scores = all_scores(query_heads, key_heads)
        top = jnp.max(scores, axis=-1, keepdims=True)
        weights = jnp.where(live_keys, jnp.exp(scores - top), 0.0)
        total = jnp.sum(weights, axis=-1, keepdims=True)
        added = jnp.einsum(
            "hsp,phd->hsd", weights.astype(half), value_heads, preferred_element_type=single
        )
        log_total = top + jnp.log(total)
        attn = (added / total).transpose(1, 0, 2).reshape(seq_rows, width_part).astype(half)

        attn_proj = swap_sum(attn, full_out, ((1,), (1,))) + bias_out
        hidden1 = (x_full + scale1 * attn_proj).astype(half)
        hidden_wide = hidden1.astype(single)
        normed2, inv2 = normalize(hidden_wide)
        act2 = (normed2 * gain2 + shift2).astype(half)
        pre = dot(act2, full_fc1, ((1,), (0,))) + b_fc1.astype(single)
        inner = jax.nn.gelu(pre, approximate=False).astype(half)

        grad_mlp = (grad_y * scale2).astype(half)
        g_bfc2 = jnp.sum(grad_y * scale2, axis=0)

        def column_parts(left, right, parts):
            step = right.shape[1] // parts
            mid = left.shape[1] // 2
            made = []
            for k in range(parts):
                columns = right[:, k * step : (k + 1) * step]

                def make_half(which, columns=columns):
                    rows = left[:, mid:] if which else left[:, :mid]
                    return dot(rows, columns, ((0,), (0,)))

                made.append(scatter_rows(make_half, 0))
            return jnp.concatenate(made, axis=1) if parts > 1 else made[0]

        g_wfc2 = column_parts(grad_mlp, inner, 2)

        mlp = swap_sum(inner, full_fc2, ((1,), (1,))) + bias_fc2
        result = own_features((hidden_wide + scale2 * mlp).astype(half))
        g_ls2 = jnp.sum(grad_y * mlp, axis=0)

        grad_inner = dot(grad_mlp, full_fc2, ((1,), (0,)))
        grad_pre = grad_inner * gelu_slope(pre)
        g_bfc1 = jnp.sum(grad_pre, axis=0)
        grad_pre_half = grad_pre.astype(half)
        g_wfc1 = column_parts(act2, grad_pre_half, 2)
        grad_act2 = swap_sum(grad_pre_half, full_fc1, ((1,), (1,)))
        g_ln2g = jnp.sum(grad_act2 * normed2, axis=0)
        g_ln2b = jnp.sum(grad_act2, axis=0)
        grad_h1 = grad_y + normalize_back(grad_act2 * gain2, normed2, inv2)
        g_ls1 = jnp.sum(grad_h1 * attn_proj, axis=0)
        g_bout = jnp.sum(grad_h1 * scale1, axis=0)
        grad_proj = (grad_h1 * scale1).astype(half)
        grad_attn = dot(grad_proj, full_out, ((1,), (0,))).astype(half)
        g_wout = column_parts(grad_proj, attn, 1)

        grad_heads = grad_attn.reshape(seq_rows, heads_part, HD)
        attn_heads = attn.reshape(seq_rows, heads_part, HD)
        row_dots = jnp.einsum(
            "shd,shd->hs", grad_heads, attn_heads, preferred_element_type=single
        )
        scores = all_scores(query_heads, key_heads)
        probs = jnp.where(live_keys, jnp.exp(scores - log_total), 0.0)
        grad_probs = jnp.einsum(
            "shd,phd->hsp", grad_heads, value_heads, preferred_element_type=single
        )
        grad_scores = (probs * (grad_probs - row_dots[..., None])).astype(half)
        grad_query = jnp.einsum(
            "hsp,phd->shd", grad_scores, key_heads, preferred_element_type=single
        )
        grad_keys = jnp.einsum(
            "hsp,shd->phd", grad_scores, query_heads, preferred_element_type=single
        ).reshape(count, width_part)
        grad_values = jnp.einsum(
            "hsp,shd->phd", probs.astype(half), grad_heads, preferred_element_type=single
        ).reshape(count, width_part)
        grad_kv = jnp.stack([grad_keys, grad_values])
        own = grad_kv[:, :seq_rows]
        for step in range(1, n_ctx):
            part = grad_kv[:, step * seq_rows : (step + 1) * seq_rows].astype(half)
            own = own + from_ctx(part, n_ctx - step).astype(single)
        grad_q = grad_query.reshape(seq_rows, width_part) * softmax_scale
        g_bqv = jnp.stack([jnp.sum(grad_q, axis=0), jnp.sum(own[1], axis=0)])
        grad_qkv = jnp.concatenate([grad_q[None], own]).astype(half)
        flat = jnp.concatenate([grad_qkv[0], grad_qkv[1], grad_qkv[2]], axis=1)
        g_wqkv = column_parts(act1, flat, 1)
        g_wqkv = jnp.stack([g_wqkv[:, c * width_part : (c + 1) * width_part] for c in range(3)])
        flat_qkv = jnp.concatenate([full_qkv[0], full_qkv[1], full_qkv[2]], axis=1)
        grad_act1 = swap_sum(flat, flat_qkv, ((1,), (1,)))
        g_ln1g = jnp.sum(grad_act1 * normed1, axis=0)
        g_ln1b = jnp.sum(grad_act1, axis=0)
        in_grad = own_features(
            (grad_h1 + normalize_back(grad_act1 * gain1, normed1, inv1)).astype(half)
        )

        def feature_order(vectors):
            return lax.dot_general(
                jnp.stack(vectors), plain.astype(single), (((1,), (1,)), ((), ())),
                precision=lax.Precision.HIGHEST, preferred_element_type=single,
            )

        def everywhere(values):
            return doubling(
                doubling(values, "fsdp", n_fsdp, single), "ctx", n_ctx, single
            )

        def own_half(values):
            return lax.dynamic_slice_in_dim(values, tp_index * width_part, width_part, 0)

        early = everywhere(
            jnp.concatenate(
                [
                    feature_order([g_ln2g, g_ln2b, g_ls1, g_bout, g_ls2, g_bfc2]).reshape(-1),
                    g_bfc1,
                ]
            )
        )
        late = everywhere(
            jnp.concatenate(
                [feature_order([g_ln1g, g_ln1b]).reshape(-1), g_bqv.reshape(-1)]
            )
        )
        rows = [early[k * width : (k + 1) * width] for k in range(6)]
        return (
            result[None],
            in_grad[None],
            g_wqkv,
            late[2 * width :].reshape(2, width_part),
            g_wout,
            own_half(rows[3]),
            late[:width],
            late[width : 2 * width],
            rows[0],
            rows[1],
            g_wfc1,
            early[6 * width :],
            g_wfc2,
            own_half(rows[5]),
            own_half(rows[2]),
            own_half(rows[4]),
        )

    return body


def solution(mesh):
    placed = (
        P("fsdp", "ctx", "tp"),
        P(None, "fsdp", "tp"),
        P(None, "tp"),
        P("fsdp", "tp"),
        P("tp"),
        P(),
        P(),
        P(),
        P(),
        P("fsdp", "tp"),
        P("tp"),
        P("fsdp", "tp"),
        P("tp"),
        P("tp"),
        P("tp"),
        P("fsdp"),
        P("fsdp", "ctx", "tp"),
    )
    return jax.shard_map(
        make_body(mesh.shape["fsdp"], mesh.shape["ctx"]),
        mesh=mesh,
        in_specs=placed,
        out_specs=(
            P("fsdp", "ctx", "tp"),
            P("fsdp", "ctx", "tp"),
            P(None, "fsdp", "tp"),
            P(None, "tp"),
            P("fsdp", "tp"),
            P("tp"),
            P(),
            P(),
            P(),
            P(),
            P("fsdp", "tp"),
            P("tp"),
            P("fsdp", "tp"),
            P("tp"),
            P("tp"),
            P("tp"),
        ),
        check_vma=False,
    )
```

```python
import functools

import jax
import jax.numpy as jnp
from jax import lax
from jax.experimental import pallas as pl
from jax.experimental.pallas import tpu as pltpu
from jax.sharding import PartitionSpec as P


HD = 64
norm_eps = 1e-06
root_half = 0.7071067811865476
inv_root_two_pi = 0.3989422804014327
single = jnp.float32
half = jnp.bfloat16


def head_mask(shape, which):
    lane = lax.broadcasted_iota(jnp.int32, shape, len(shape) - 1)
    return (lane < HD) if which == 0 else (lane >= HD)


def pick(values, which):
    return jnp.where(head_mask(values.shape, which), values, jnp.zeros_like(values))


def attend_kernel(q_ref, k_ref, v_ref, bias_ref, out_ref, log_ref):
    queries, keys, values = q_ref[...], k_ref[...], v_ref[...]
    outs, logs = [], []
    for which in range(2):
        scores = lax.dot_general(pick(queries, which), keys, (((1,), (1,)), ((), ())),
                                 preferred_element_type=single) + bias_ref[...]
        top = jnp.max(scores, axis=-1, keepdims=True)
        weights = jnp.exp(scores - top)
        total = jnp.sum(weights, axis=-1, keepdims=True)
        added = jnp.dot(weights.astype(half), values, preferred_element_type=single)
        outs.append(added / total)
        logs.append(top + jnp.log(total))
    low = head_mask(outs[0].shape, 0)
    out_ref[...] = jnp.where(low, outs[0], outs[1]).astype(half)
    log_ref[...] = jnp.where(low, logs[0], logs[1])


def attend_more_kernel(q_ref, k_ref, v_ref, bias_ref, _, __, out_ref, log_ref):
    attend_kernel(q_ref, k_ref, v_ref, bias_ref, out_ref, log_ref)


def attend(mixed, rows, bias, first, pairs, before=()):
    count, width = mixed.shape[0], mixed.shape[1] // 3
    lanes = 2 * HD
    all_pairs = width // lanes
    kept = pl.BlockSpec(memory_space=pl.ANY)
    return pl.pallas_call(
        attend_more_kernel if before else attend_kernel,
        grid=(pairs,),
        in_specs=[
            pl.BlockSpec((rows, lanes), lambda p: (0, first + p)),
            pl.BlockSpec((count, lanes), lambda p: (0, all_pairs + first + p)),
            pl.BlockSpec((count, lanes), lambda p: (0, 2 * all_pairs + first + p)),
            pl.BlockSpec((1, count), lambda p: (0, 0)),
        ]
        + [kept] * len(before),
        out_specs=[pl.BlockSpec((rows, lanes), lambda p: (0, first + p))] * 2,
        out_shape=[
            jax.ShapeDtypeStruct((rows, width), half),
            jax.ShapeDtypeStruct((rows, width), single),
        ],
        input_output_aliases={4: 0, 5: 1} if before else {},
        cost_estimate=pl.CostEstimate(
            flops=32 * rows * count * pairs * lanes,
            bytes_accessed=6 * (rows + count) * pairs * lanes,
            transcendentals=rows * count * pairs * 2,
        ),
        name="attend",
    )(mixed, mixed, mixed, bias, *before)


def attend_back_kernel(
    scale, q_ref, k_ref, v_ref, bias_ref, log_ref, out_ref, grad_ref, dq_ref, dk_ref, dv_ref, sum_ref
):
    queries, keys, values, grads = q_ref[...], k_ref[...], v_ref[...], grad_ref[...]
    log_rows = jnp.transpose(log_ref[...])
    products = grads.astype(single) * out_ref[...].astype(single)
    ones = jnp.ones((8, 2 * HD), single)
    keys_turned = jnp.transpose(keys)
    sub = lax.broadcasted_iota(jnp.int32, keys_turned.shape, 0)
    dk = dv = dq = None
    for which in range(2):
        q_h, g_h = pick(queries, which), pick(grads, which)
        scores = lax.dot_general(
            keys, q_h, (((1,), (1,)), ((), ())), preferred_element_type=single
        )
        log_row = log_rows[which * HD : which * HD + 1, :]
        probs = jnp.exp(scores + bias_ref[...] - log_row)
        row_dots = lax.dot_general(
            pick(ones, which), products, (((1,), (1,)), ((), ())),
            precision=lax.Precision.HIGHEST, preferred_element_type=single,
        )[:1]
        grad_probs = lax.dot_general(
            values, g_h, (((1,), (1,)), ((), ())), preferred_element_type=single
        )
        grad_scores = (probs * (grad_probs - row_dots)).astype(half)
        dv_h = jnp.dot(probs.astype(half), g_h, preferred_element_type=single)
        dk_h = jnp.dot(grad_scores, q_h, preferred_element_type=single)
        own_rows = (sub < HD) if which == 0 else (sub >= HD)
        k_h = jnp.where(own_rows, keys_turned, jnp.zeros_like(keys_turned))
        dq_h = jnp.dot(k_h, grad_scores, preferred_element_type=single)
        dk, dv, dq = (dk_h, dv_h, dq_h) if dk is None else (dk + dk_h, dv + dv_h, dq + dq_h)
    dq = jnp.transpose(dq) * scale
    dq_ref[...] = dq.astype(half)
    dk_ref[...] = dk.astype(half)
    dv_ref[...] = dv.astype(half)
    sum_q = jnp.sum(dq, axis=0, keepdims=True)
    sum_v = jnp.sum(dv, axis=0, keepdims=True)
    first = lax.broadcasted_iota(jnp.int32, (8, 2 * HD), 0) == 0
    sum_ref[...] = jnp.where(first, sum_q, sum_v)


def attend_back(mixed, rows, bias, logs, attn, grads, scale, first, pairs):
    count, width = mixed.shape[0], mixed.shape[1] // 3
    lanes = 2 * HD
    all_pairs = width // lanes
    part = pairs * lanes
    short = pl.BlockSpec((rows, lanes), lambda p: (0, first + p))
    made = pl.BlockSpec((rows, lanes), lambda p: (0, p))
    tall = pl.BlockSpec((count, lanes), lambda p: (0, p))
    return pl.pallas_call(
        functools.partial(attend_back_kernel, scale),
        grid=(pairs,),
        in_specs=[
            short,
            pl.BlockSpec((count, lanes), lambda p: (0, all_pairs + first + p)),
            pl.BlockSpec((count, lanes), lambda p: (0, 2 * all_pairs + first + p)),
            pl.BlockSpec((count, 1), lambda p: (0, 0)),
            short, short, short,
        ],
        out_specs=[made, tall, tall, pl.BlockSpec((8, lanes), lambda p: (0, p))],
        out_shape=[
            jax.ShapeDtypeStruct((rows, part), half),
            jax.ShapeDtypeStruct((count, part), half),
            jax.ShapeDtypeStruct((count, part), half),
            jax.ShapeDtypeStruct((8, part), single),
        ],
        cost_estimate=pl.CostEstimate(
            flops=80 * rows * count * part,
            bytes_accessed=12 * (rows + count) * part,
            transcendentals=rows * count * part // HD,
        ),
        name="attend_back",
    )(mixed, mixed, mixed, bias, logs, attn, grads)


FSDP, CTX, TP = "fsdp", "ctx", "tp"


def dot(left, right, dims):
    return lax.dot_general(left, right, (dims, ((), ())), preferred_element_type=single)


def gate(value, *earlier):
    return lax.optimization_barrier((value,) + earlier)[0]


def both_dot(pair, weights):
    return dot(pair[0], weights[0], ((1,), (0,))) + dot(pair[1], weights[1], ((1,), (0,)))


def normalize(pair):
    width = 2 * pair[0].shape[-1]
    average = sum(jnp.sum(part, axis=-1, keepdims=True) for part in pair) / width
    centred = [part - average for part in pair]
    spread = sum(jnp.sum(part * part, axis=-1, keepdims=True) for part in centred) / width
    inv_std = lax.rsqrt(spread + norm_eps)
    return [part * inv_std for part in centred], inv_std


def normalize_back(grad_normed, normed, inv_std):
    width = 2 * normed[0].shape[-1]
    first = sum(jnp.sum(g, axis=-1, keepdims=True) for g in grad_normed) / width
    second = sum(jnp.sum(g * n, axis=-1, keepdims=True) for g, n in zip(grad_normed, normed)) / width
    return [inv_std * (g - first - n * second) for g, n in zip(grad_normed, normed)]


def column_sum(values):
    return jnp.sum(values, axis=0)


def place_kernel(spots_ref, *refs):
    out_ref = refs[-1]
    rows = refs[0].shape[0]
    for k, ref in enumerate(refs[:-1]):
        start = pl.multiple_of(spots_ref[k] * rows, 16)
        out_ref[pl.ds(start, rows), :] = ref[...]


def place_blocks(spots, blocks):
    rows, columns = blocks[0].shape
    whole = pl.BlockSpec(memory_space=pltpu.VMEM)
    return pl.pallas_call(
        place_kernel,
        in_specs=[pl.BlockSpec(memory_space=pltpu.SMEM)] + [whole] * len(blocks),
        out_specs=whole,
        out_shape=jax.ShapeDtypeStruct((len(blocks) * rows, columns), blocks[0].dtype),
        cost_estimate=pl.CostEstimate(
            flops=0, bytes_accessed=4 * len(blocks) * rows * columns, transcendentals=0
        ),
        name="place",
    )(spots, *blocks)


def make_body(n_fsdp, n_ctx):
    n_line = n_fsdp // 2
    lines = [[line * 2 + pair for line in range(n_line)] for pair in range(2)]

    def pair_swap(values):
        return lax.ppermute(values, FSDP, [(i, i ^ 1) for i in range(n_fsdp)])

    def tp_swap(values):
        return lax.ppermute(values, TP, [(0, 1), (1, 0)])

    def from_ctx(values, step):
        return lax.ppermute(values, CTX, [((i + step) % n_ctx, i) for i in range(n_ctx)])

    def doubling(values, axis, count, link):
        step = 1
        while step < count:
            sent = values.astype(link)
            other = lax.ppermute(sent, axis, [(i, i ^ step) for i in range(count)])
            values = sent.astype(single) + other.astype(single)
            step *= 2
        return values

    def from_line(values, step):
        return lax.ppermute(
            values,
            FSDP,
            [
                (((line + step) % n_line) * 2 + pair, line * 2 + pair)
                for line in range(n_line)
                for pair in range(2)
            ],
        )

    steps = sorted(range(1, n_line), key=lambda s: min(s, n_line - s))

    def line_gather(shard):
        return lax.all_gather(shard, FSDP, axis=0, tiled=True, axis_index_groups=lines)

    def line_scatter(values):
        return lax.psum_scatter(
            values, FSDP, scatter_dimension=0, tiled=True, axis_index_groups=lines
        )

    def total_pair(parts):
        return [part + other for part, other in zip(parts, [tp_swap(part) for part in parts])]

    def body(
        inputs, w_qkv, b_qv, w_out, b_out, ln1_gain, ln1_bias, ln2_gain, ln2_bias,
        w_fc1, b_fc1, w_fc2, b_fc2, ls1, ls2, lengths, out_grad,
    ):
        seq_rows, width_part = inputs.shape[1], inputs.shape[2]
        width = 2 * width_part
        mid = width // 2
        cut = w_fc1.shape[1] // n_ctx
        softmax_scale = HD ** (-0.5)
        tp_index = lax.axis_index(TP)
        ctx_index = lax.axis_index(CTX)
        place = lax.axis_index(FSDP)
        pair, line = place % 2, place // 2
        parts = range(n_ctx)

        def hidden_block(values, step, axis):
            start = ((ctx_index + step) % n_ctx) * cut
            return lax.dynamic_slice_in_dim(values, start, cut, axis)

        def hidden_order(blocks, axis):
            placed = [
                sum(jnp.where((ctx_index + r) % n_ctx == j, blocks[r], 0.0) for r in parts)
                for j in parts
            ]
            return jnp.concatenate(placed, axis=axis)

        def line_blocks(shard):
            blocks = {0: shard}
            for step in steps:
                blocks[step] = from_line(shard, step)
            return blocks

        def placed_rows(blocks):
            spots = (line + jnp.arange(n_line, dtype=jnp.int32)) % n_line
            return place_blocks(spots, [blocks[step] for step in range(n_line)])

        def swap_blocks(blocks, *earlier):
            swapped = {}
            for step, block in blocks.items():
                swapped[step] = pair_swap(gate(block, *earlier) if earlier and step else block)
            return swapped

        own_qkv = jnp.concatenate([w_qkv[0], w_qkv[1], w_qkv[2]], axis=1)
        block_rows = own_qkv.shape[0]
        qkv_blocks = line_blocks(own_qkv)
        out_blocks = line_blocks(w_out)
        near, weight = {}, {}
        for name, shard in (
            ("u0", hidden_block(w_fc1, 0, 1)),
            ("d0", hidden_block(w_fc2, 0, 1)),
        ):
            near[name] = line_gather(gate(shard, *[qkv_blocks[step] for step in steps]))

        def fetch(name, *earlier):
            near_rows = near[name]
            far_rows = pair_swap(gate(near_rows, *earlier) if earlier else near_rows)
            weight[name] = (near_rows, far_rows)

        def spread(name, side, *earlier):
            rows = gate(weight[name + "0"][side], *earlier)
            return [from_ctx(rows, r) for r in parts[1:]]

        slot = jnp.arange(width, dtype=jnp.int32)
        member = pair ^ (slot // mid)
        line_of = (slot % mid) // block_rows
        feature = (line_of * 2 + member) * block_rows + slot % block_rows
        own_first = (slot + tp_index * width_part) % width
        select = (own_first[:, None] == feature[None, :]).astype(half)
        plain = (slot[:, None] == feature[None, :]).astype(half)

        def halves(values):
            return [values[:, :mid], values[:, mid:]]

        def to_device_order(own):
            both = jnp.concatenate([own, tp_swap(own)], axis=1)
            return [dot(both, part, ((1,), (0,))) for part in halves(select)]

        def own_features(values):
            turned = halves(select[:width_part])
            return sum(dot(v, t, ((1,), (1,))) for v, t in zip(values, turned)).astype(half)

        x_full = to_device_order(inputs[0])
        ctx_rows = [from_ctx(inputs[0], step) for step in range(1, n_ctx)]
        x_rest = to_device_order(jnp.concatenate(ctx_rows, axis=0))
        grad_y = to_device_order(out_grad[0])
        small_own = jnp.concatenate(to_device_order(jnp.stack([b_out, b_fc2, ls1, ls2])), axis=1)
        bias_out, bias_fc2, scale1, scale2 = [halves(small_own[i : i + 1]) for i in range(4)]
        small_all = dot(
            jnp.stack([ln1_gain, ln1_bias, ln2_gain, ln2_bias]), plain, ((1,), (0,))
        )
        gain1, shift1, gain2, shift2 = [halves(small_all[i : i + 1]) for i in range(4)]

        def first_act(rows):
            normed, inv_std = normalize(rows)
            act = [(n * g + t).astype(half) for n, g, t in zip(normed, gain1, shift1)]
            return normed, inv_std, act

        normed1, inv1, act_own = first_act(x_full)
        _, _, act_rest = first_act(x_rest)
        act_all = [jnp.concatenate([o, r], axis=0) for o, r in zip(act_own, act_rest)]
        qkv_swapped = swap_blocks(qkv_blocks)
        w_mixed = [placed_rows(qkv_blocks), placed_rows(qkv_swapped)]
        bias_row = jnp.concatenate(
            [b_qv[0], jnp.zeros_like(b_qv[0]), b_qv[1]]
        ).astype(single)
        scale_row = jnp.where(jnp.arange(3 * width_part) < width_part, softmax_scale, 1.0)
        mixed = ((both_dot(act_all, w_mixed) + bias_row) * scale_row.astype(single)).astype(half)
        count = n_ctx * seq_rows
        at = jnp.arange(count, dtype=jnp.int32)
        positions = ((ctx_index + at // seq_rows) % n_ctx) * seq_rows + at % seq_rows
        bias = jnp.where(positions < lengths[0], 0.0, -1e30).astype(single)

        out_swapped = swap_blocks(out_blocks, mixed)
        some = width_part // (4 * HD)
        begun = attend(mixed, seq_rows, bias[None, :], 0, some)
        fetch("u0", begun[0])
        fc1_near = spread("u", 0, begun[0])
        attn, logs = attend(
            mixed, seq_rows, bias[None, :], some, width_part // (2 * HD) - some, tuple(begun)
        )

        fetch("d0", attn)
        fc2_near = spread("d", 0, attn)
        for r in parts[1:]:
            near["u%d" % r] = fc1_near[r - 1]
            fetch("u%d" % r, attn)
        weight["out"] = [placed_rows(out_blocks), placed_rows(out_swapped)]

        partial = [dot(attn, w, ((1,), (1,))) for w in weight["out"]]
        attn_proj = [p + b for p, b in zip(total_pair(partial), bias_out)]
        hidden1 = [(x + s * p).astype(half) for x, s, p in zip(x_full, scale1, attn_proj)]
        hidden_wide = [h.astype(single) for h in hidden1]
        normed2, inv2 = normalize(hidden_wide)
        act2 = [(n * g + s).astype(half) for n, g, s in zip(normed2, gain2, shift2)]
        grad_mlp = [(g * s).astype(half) for g, s in zip(grad_y, scale2)]
        g_bfc2 = jnp.concatenate([column_sum(g * s) for g, s in zip(grad_y, scale2)])

        def hidden_part(name, bias_part):
            pre = both_dot(act2, weight[name]) + bias_part.astype(single)
            share = 0.5 * (1.0 + lax.erf(pre * root_half))
            slope = share + pre * inv_root_two_pi * jnp.exp(-0.5 * pre * pre)
            return (pre * share).astype(half), slope

        def send_far(left, right):
            return pair_swap(dot(left[1], right, ((0,), (0,))).astype(half))

        def take_near(left, right, came):
            kept = dot(left[0], right, ((0,), (0,)))
            return line_scatter((kept + came.astype(single)).astype(half))

        def finish(owned):
          return doubling(owned.astype(single), CTX, n_ctx, half)

        inner, slope, grad_pre, fc2_came = {}, {}, {}, []
        inner[0], slope[0] = hidden_part("u0", hidden_block(b_fc1, 0, 0))
        fc2_far = spread("d", 1, inner[0])
        for r in parts[1:]:
            weight["d%d" % r] = (fc2_near[r - 1], fc2_far[r - 1])
        grad_pre[0] = both_dot(grad_mlp, weight["d0"]) * slope[0]
        came_fc1 = {0: send_far(act2, grad_pre[0].astype(half))}
        for r in parts[1:]:
            inner[r], slope[r] = hidden_part("u%d" % r, hidden_block(b_fc1, r, 0))
            for side in (1, 0):
                block = dot(grad_mlp[side], inner[r], ((0,), (0,))).astype(half)
                fc2_came.append((side, from_ctx(block, n_ctx - r)))
            grad_pre[r] = both_dot(grad_mlp, weight["d%d" % r]) * slope[r]
            came_fc1[r] = send_far(act2, grad_pre[r].astype(half))
        g_bfc1 = hidden_order([column_sum(grad_pre[r]) for r in parts], 0)
        grad_hid = [grad_pre[r].astype(half) for r in parts]
        grad_act2 = total_pair(
            [
                sum(dot(grad_hid[r], weight["u%d" % r][side], ((1,), (1,))) for r in parts)
                for side in range(2)
            ]
        )
        owned_fc1 = {}
        owned_fc1[0] = take_near(act2, grad_hid[0], gate(came_fc1[0], grad_hid[-1]))
        back = normalize_back([g * n for g, n in zip(grad_act2, gain2)], normed2, inv2)
        grad_h1 = [g + b for g, b in zip(grad_y, back)]
        grad_proj = [(g * s).astype(half) for g, s in zip(grad_h1, scale1)]

        def fc2_sum(side, *earlier):
            total = dot(grad_mlp[side], inner[0], ((0,), (0,)))
            for where, block in fc2_came:
                if where == side:
                    total = total + gate(block, *earlier).astype(single)
            return total

        came_fc2 = pair_swap(fc2_sum(1, grad_proj[0]).astype(half))
        grad_attn = both_dot(grad_proj, weight["out"]).astype(half)
        came_out = send_far(grad_proj, attn)
        for r in parts[1:]:
            came = gate(came_fc1[r], grad_attn)
            owned_fc1[r] = take_near(act2, grad_hid[r], came)

        def send_qkv(made):
            far = [dot(a[1], g, ((0,), (0,))).astype(half) for a, g in zip(acts, made)]
            return pair_swap(jnp.concatenate(far, axis=1)), far[-1]

        acts = (act_own, act_all, act_all)
        grads, sums_parts, came_qkv = [], [], []
        for first in (0, some):
            *made, sums = attend_back(
                mixed, seq_rows, bias[:, None], logs, attn,
                gate(grad_attn, grads[0][0]) if first else grad_attn, softmax_scale,
                first, some if first == 0 else width_part // (2 * HD) - some,
            )
            grads.append(made)
            sums_parts.append(sums)
            came, sent = send_qkv(made)
            came_qkv.append(came)
        sums_qv = jnp.concatenate(sums_parts, axis=1)

        def line_sum(made, came):
            kept = [dot(a[0], g, ((0,), (0,))) for a, g in zip(acts, made)]
            total = jnp.concatenate(kept, axis=1) + came.astype(single)

            def block(step):
                start = ((line + step) % n_line) * block_rows
                return lax.dynamic_slice_in_dim(total, start, block_rows, 0)

            own = block(0)
            for step in steps:
                own = own + from_line(block(step).astype(half), n_line - step).astype(single)
            return own, total

        kv_grads = jnp.concatenate(
            [grads[0][1], grads[1][1], grads[0][2], gate(grads[1][2], sent)], axis=1
        )
        kv_terms = [dot(kv_grads, w[:, width_part:], ((1,), (1,))) for w in w_mixed]
        rest = [terms[seq_rows:] for terms in kv_terms]
        mine = jnp.where(tp_index == 0, rest[0], rest[1])
        theirs = jnp.where(tp_index == 0, rest[1], rest[0])
        mine = mine + tp_swap(theirs)
        arrived = 0.0
        mine = mine.astype(half)
        for step in range(1, n_ctx):
            part = mine[(step - 1) * seq_rows : step * seq_rows]
            arrived = arrived + from_ctx(part, n_ctx - step).astype(single)
        far_sum = gate(came_fc2, mine).astype(single)
        owned_fc2 = line_scatter((fc2_sum(0, mine) + far_sum).astype(half))
        owned_out = take_near(grad_proj, attn, gate(came_out, mine))
        owned_qkv_a, total_a = line_sum(grads[0], gate(came_qkv[0], mine))
        late = [gate(inner[r], total_a) for r in parts]
        partial = [
            sum(dot(late[r], weight["d%d" % r][side], ((1,), (1,))) for r in parts)
            for side in range(2)
        ]
        swapped_mlp = [tp_swap(part) for part in partial]
        owned_qkv_b, total_b = line_sum(grads[1], gate(came_qkv[1], *partial))
        owned_qkv = [owned_qkv_a, owned_qkv_b]
        mlp = [
            p + gate(o, total_b) + b for p, o, b in zip(partial, swapped_mlp, bias_fc2)
        ]
        result = own_features(
            [(h + s * m).astype(half) for h, s, m in zip(hidden_wide, scale2, mlp)]
        )
        q_grads = gate(jnp.concatenate([grads[0][0], grads[1][0]], axis=1), total_b)
        partial1 = [
          dot(q_grads, w[:, :width_part], ((1,), (1,))) + terms[:seq_rows]
          + jnp.where(tp_index == side, arrived, 0.0)
          for side, (w, terms) in enumerate(zip(w_mixed, kv_terms))
        ]
        grad_act1 = total_pair(partial1)
        back = normalize_back([g * n for g, n in zip(grad_act1, gain1)], normed1, inv1)
        in_grad = own_features([(g + b).astype(half) for g, b in zip(grad_h1, back)])

        def joined_sum(left, right):
            return jnp.concatenate([column_sum(a * b) for a, b in zip(left, right)])

        def joined(parts):
            return jnp.concatenate([column_sum(part) for part in parts])

        def feature_order(vectors):
            return lax.dot_general(
                jnp.stack(vectors), plain.astype(single), (((1,), (1,)), ((), ())),
                precision=lax.Precision.HIGHEST, preferred_element_type=single,
            )

        def everywhere(values):
            return doubling(
                doubling(values, FSDP, n_fsdp, single), CTX, n_ctx, single
            )

        def own_half(values):
            return lax.dynamic_slice_in_dim(values, tp_index * width_part, width_part, 0)

        local = (
            jnp.concatenate(
                [
                    feature_order(
                        [
                            joined_sum(grad_act2, normed2), joined(grad_act2),
                            joined_sum(grad_h1, attn_proj), joined_sum(grad_h1, scale1),
                            joined_sum(grad_y, mlp), g_bfc2,
                            joined_sum(grad_act1, normed1), joined(grad_act1),
                        ]
                    ).reshape(-1),
                    g_bfc1, sums_qv[0], sums_qv[1],
                ]
            )
        )
        sums = everywhere(local)
        rows = [sums[k * width : (k + 1) * width] for k in range(8)]
        tail = sums[8 * width :]
        hidden = g_bfc1.shape[0]
        done_qkv = [finish(gate(block, local)) for block in owned_qkv]
        g_wqkv = jnp.stack(
            [
                jnp.concatenate(
                    [done[:, c * (done.shape[1] // 3) : (c + 1) * (done.shape[1] // 3)] for done in done_qkv],
                    axis=1,
                )
                for c in range(3)
            ]
        )
        owned_fc2 = gate(owned_fc2, local)
        all_fc2 = [owned_fc2] + [from_ctx(owned_fc2, r) for r in parts[1:]]
        g_wfc2 = hidden_order([block.astype(single) for block in all_fc2], 1)
        return (
            result[None],
            in_grad[None],
            g_wqkv,
            tail[hidden:].reshape(2, width_part),
            finish(gate(owned_out, local)),
            own_half(rows[3]),
            rows[6],
            rows[7],
            rows[0],
            rows[1],
            finish(hidden_order([owned_fc1[r].astype(single) for r in parts], 1)),
            tail[:hidden],
            g_wfc2,
            own_half(rows[5]),
            own_half(rows[2]),
            own_half(rows[4]),
        )

    return body


def solution(mesh):
    placed = (
        P(FSDP, CTX, TP),
        P(None, FSDP, TP),
        P(None, TP),
        P(FSDP, TP),
        P(TP),
        P(),
        P(),
        P(),
        P(),
        P(FSDP, TP),
        P(TP),
        P(FSDP, TP),
        P(TP),
        P(TP),
        P(TP),
        P(FSDP),
        P(FSDP, CTX, TP),
    )
    plain_body = make_body(mesh.shape[FSDP], mesh.shape[CTX])

    return jax.shard_map(
        plain_body,
        mesh=mesh,
        in_specs=placed,
        out_specs=(
            P(FSDP, CTX, TP),
            P(FSDP, CTX, TP),
            P(None, FSDP, TP),
            P(None, TP),
            P(FSDP, TP),
            P(TP),
            P(),
            P(),
            P(),
            P(),
            P(FSDP, TP),
            P(TP),
            P(FSDP, TP),
            P(TP),
            P(TP),
            P(TP),
        ),
        check_vma=False,
    )
```
